512 devices in a mesh: band: 8 (over y_lo, core), row: 64 (over z, x, y_hi).
Axes of the slice: x: 4, y: 8 (y_hi: 2, y_lo: 4; y = y_hi * 4 + y_lo), z: 8, core: 2. Of those that a mesh axis runs over, the one named last changes fastest.
Arguments:
- pixels: float32 [512, 64, 7168], P('row', None, 'band'), may hold values from -6 to 6
- embed_weight: float32 [64, 64], replicated, may hold values from -0.75 to 0.75
- band_position_embedding: float32 [112, 64], replicated, may hold values from -6 to 6
- spec_qkv: float32 [64, 192], replicated, may hold values from -0.75 to 0.75
- spec_out: float32 [64, 64], replicated, may hold values from -0.75 to 0.75
- spec_scale: float32 [4], replicated, may hold values from 0.5 to 300, as said below
- spectral_up_weight: float32 [64, 256], replicated, may hold values from -0.75 to 0.75
- spectral_down_weight: float32 [256, 64], replicated, may hold values from -0.375 to 0.375
- pool_weight: float32 [12, 112], replicated, may hold values from -0.5 to 0.5
- qkv_weight: float32 [768, 2304], P(None, 'band'), may hold values from -0.21875 to 0.21875
- out_weight: float32 [768, 768], P(None, 'band'), may hold values from -0.21875 to 0.21875
- spat_scale: float32 [12], replicated, may hold values from 0.5 to 300, as said below
- shifts: int32 [2], replicated, may hold values from 1 to 7, as said below
Outputs:
- patch_out: float32 [512, 64, 768], P('row', 'band')
The draws below stay inside these ranges and needn't reach their ends.
Inputs may be any that keep to these rules, and one draw needn't show every extreme that they name: shifts[0] rolls patch rows and lies in 1 to 7; shifts[1] rolls patch columns and lies in 1 to 7; the shift along the longer of the two (rows where 8 >= 8) is at its upper end. `spec_scale`: one positive scale per head. `spat_scale`: one positive scale per head.
All inputs are finite; a program needn't handle non-finite values.
Results may differ from the reference program's by a relative error of at most 0.0003.
Values sent between devices are 32-bit elements; how exact they have to be, the bound alone decides.
A program may use at most 64 MiB of HBM per device.

```python
import math
import jax
import jax.numpy as jnp
from jax import lax

BANDS = 112
PIX = 64
SW = 64
SHEADS = 4
SFF = 256
D = 768
HEADS = 12
WIN = 8
PR = 8
PC = 8
PROWS = 512
PCOLS = 64
GROUPS = 12


def scale_draw(key, head_count, lowest, largest):
    unit = jax.random.uniform(key, (head_count,), jnp.float32)
    return jnp.exp(jnp.log(lowest) + unit * (jnp.log(largest) - jnp.log(lowest)))


def draw_spec_scale(key, part):
    return scale_draw(key, SHEADS, 0.5, 2.0)


def draw_spat_scale(key, part):
    return scale_draw(key, HEADS, 0.5, 2.0)


def draw_shifts(key, part):
    row_key = jax.random.fold_in(key, 11)
    col_key = jax.random.fold_in(key, 23)
    row_shift = jax.random.randint(row_key, (1,), 1, PR, dtype=jnp.int32)
    col_shift = jax.random.randint(col_key, (1,), 1, PC, dtype=jnp.int32)
    if PR >= PC:
        row_shift = jnp.full((1,), PR - 1, jnp.int32)
    else:
        col_shift = jnp.full((1,), PC - 1, jnp.int32)
    return jnp.concatenate([row_shift, col_shift], 0)


def shard_levels(key, shape, pieces, least, top_value):
    level, own = 1.0, jax.random.fold_in(key, 6)
    for dim, shards_of in pieces:
        heights = jnp.exp(jax.random.uniform(jax.random.fold_in(own, dim), (shards_of,), jnp.float32, least / len(pieces), top_value / len(pieces)))
        level = level * jnp.repeat(heights, shape[dim] // shards_of).reshape([-1 if axis == dim else 1 for axis in range(len(shape))])
    return level


def bell_draw(rng, shape, scale, most, shards=(), kind=jnp.bfloat16):
    entries = jax.random.normal(rng, shape, jnp.float32) * scale
    if len(shards) > 0:
        entries = shard_levels(rng, shape, shards, -0.22, 0.18) * entries
    return jnp.clip(entries, min=-most, max=most).astype(kind)


def setup_inputs(seed: int = 0) -> dict:
    splits = jax.random.split(jax.random.key(seed), 14)
    pixels = bell_draw(splits[0], (PROWS, PCOLS, BANDS * PIX), 1.0, 6.0, ((0, 64), (2, 8)), jnp.float32)
    embed_weight = bell_draw(splits[1], (PIX, SW), PIX ** -0.5, 0.75, (), jnp.float32)
    band_position_embedding = bell_draw(splits[2], (BANDS, SW), 1.0, 6.0, (), jnp.float32)
    spec_qkv = bell_draw(splits[3], (SW, 3 * SW), SW ** -0.5, 0.75, (), jnp.float32)
    spec_out = bell_draw(splits[4], (SW, SW), SW ** -0.5, 0.75, (), jnp.float32)
    spec_scale = draw_spec_scale(jax.random.fold_in(splits[13], 71), 0)
    spectral_up_weight = bell_draw(splits[6], (SW, SFF), SW ** -0.5, 0.75, (), jnp.float32)
    spectral_down_weight = bell_draw(splits[7], (SFF, SW), SFF ** -0.5, 0.375, (), jnp.float32)
    pool_weight = bell_draw(splits[8], (GROUPS, BANDS), BANDS ** -0.5, 0.5, (), jnp.float32)
    qkv_weight = bell_draw(splits[9], (D, 3 * D), D ** -0.5, 0.21875, ((1, 8),), jnp.float32)
    out_weight = bell_draw(splits[10], (D, D), D ** -0.5, 0.21875, ((1, 8),), jnp.float32)
    spat_scale = draw_spat_scale(jax.random.fold_in(splits[13], 71), 0)
    shifts = draw_shifts(jax.random.fold_in(splits[13], 71), 0)
    return {"pixels": pixels, "embed_weight": embed_weight, "band_position_embedding": band_position_embedding, "spec_qkv": spec_qkv, "spec_out": spec_out, "spec_scale": spec_scale, "spectral_up_weight": spectral_up_weight, "spectral_down_weight": spectral_down_weight, "pool_weight": pool_weight, "qkv_weight": qkv_weight, "out_weight": out_weight, "spat_scale": spat_scale, "shifts": shifts}


highest_precision = lax.Precision.HIGHEST
epsilon = 1e-05

def layer_normalize(values):
    average = lax.optimization_barrier(jnp.mean(values, axis=-1, keepdims=True))
    centred = values - average
    spread = lax.optimization_barrier(jnp.mean(centred * centred, axis=-1, keepdims=True))
    return centred * lax.rsqrt(spread + epsilon)

def stable_softmax(scores):
    top_score = lax.optimization_barrier(jnp.max(scores, axis=-1, keepdims=True))
    shifted = jnp.exp(scores - top_score)
    return shifted / lax.optimization_barrier(jnp.sum(shifted, axis=-1, keepdims=True))

def spectral_row(patch_row, embed_weight, band_position_embedding, spec_qkv, spec_out, spec_scale, spectral_up_weight, spectral_down_weight, pool_weight):
    patch_count = patch_row.shape[0]
    band_count = band_position_embedding.shape[0]
    token_width = band_position_embedding.shape[1]
    pixel_count = embed_weight.shape[0]
    head_count = spec_scale.shape[0]
    head_size = token_width // head_count
    raw_tokens = patch_row.reshape(patch_count, band_count, pixel_count)
    tokens = jnp.einsum('cbp,pw->cbw', raw_tokens, embed_weight, precision=highest_precision) + band_position_embedding
    projected = jnp.einsum('cbw,wk->cbk', layer_normalize(tokens), spec_qkv, precision=highest_precision)
    shaped = projected.reshape(patch_count, band_count, 3, head_count, head_size)
    scores = jnp.einsum('cqhd,ckhd->chqk', shaped[:, :, 0], shaped[:, :, 1], precision=highest_precision)
    scores = scores * (spec_scale / math.sqrt(head_size))[:, None, None]
    attention = stable_softmax(scores)
    mixed = jnp.einsum('chqk,ckhd->cqhd', attention, shaped[:, :, 2], precision=highest_precision)
    mixed = mixed.reshape(patch_count, band_count, token_width)
    running_state = tokens + jnp.einsum('cbw,wv->cbv', mixed, spec_out, precision=highest_precision)
    hidden_activations = jax.nn.gelu(jnp.einsum('sio,or->sir', layer_normalize(running_state), spectral_up_weight, precision=highest_precision))
    running_state = running_state + jnp.einsum('rgp,pu->rgu', hidden_activations, spectral_down_weight, precision=highest_precision)
    pooled = jnp.einsum('gb,cbw->cgw', pool_weight, running_state, precision=highest_precision)
    return pooled.reshape(patch_count, pool_weight.shape[0] * token_width)

def to_windows(grid, window):
    grid_rows, grid_cols, feature_width = grid.shape
    shaped = grid.reshape(grid_rows // window, window, grid_cols // window, window, feature_width)
    return shaped.transpose(0, 2, 1, 3, 4).reshape(-1, window * window, feature_width)

def from_windows(windows, grid_rows, grid_cols, window):
    feature_width = windows.shape[-1]
    shaped = windows.reshape(grid_rows // window, grid_cols // window, window, window, feature_width)
    return shaped.transpose(0, 2, 1, 3, 4).reshape(grid_rows, grid_cols, feature_width)

def window_attention(projected, labels, spat_scale, window_count, window_area):
    model_width = projected.shape[1] // 3
    head_count = spat_scale.shape[0]
    head_size = model_width // head_count
    shaped = projected.reshape(window_count, window_area, 3, head_count, head_size)
    scores = jnp.einsum('wqhd,wkhd->whqk', shaped[:, :, 0], shaped[:, :, 1], precision=highest_precision)
    scores = scores * (spat_scale / math.sqrt(head_size))[:, None, None]
    same_region = labels[:, :, None] == labels[:, None, :]
    scores = jnp.where(same_region[:, None], scores, -1e+30)
    attention = stable_softmax(scores)
    mixed = jnp.einsum('whqk,wkhd->wqhd', attention, shaped[:, :, 2], precision=highest_precision)
    return mixed.reshape(window_count * window_area, model_width)

def reference(pixels, embed_weight, band_position_embedding, spec_qkv, spec_out, spec_scale, spectral_up_weight, spectral_down_weight, pool_weight, qkv_weight, out_weight, spat_scale, shifts):

    def one_row(patch_row):
        return spectral_row(patch_row, embed_weight, band_position_embedding, spec_qkv, spec_out, spec_scale, spectral_up_weight, spectral_down_weight, pool_weight)
    pooled = lax.map(one_row, pixels)
    grid_rows = pooled.shape[0]
    grid_cols = pooled.shape[1]
    model_width = pooled.shape[2]
    shift_rows = shifts[0]
    shift_cols = shifts[1]
    rolled = jnp.roll(pooled, -shift_rows, axis=0)
    rolled = jnp.roll(rolled, -shift_cols, axis=1)
    row_region = (jnp.arange(grid_rows, dtype=jnp.int32) >= grid_rows - shift_rows).astype(jnp.int32)
    col_region = (jnp.arange(grid_cols, dtype=jnp.int32) >= grid_cols - shift_cols).astype(jnp.int32)
    labels = (2 * row_region[:, None] + col_region[None, :])[:, :, None]
    windows = to_windows(rolled, WIN)
    label_windows = to_windows(labels, WIN)[:, :, 0]
    flat_tokens = windows.reshape(-1, model_width)
    projected = jnp.dot(layer_normalize(flat_tokens), qkv_weight, precision=highest_precision, preferred_element_type=jnp.float32)
    mixed = window_attention(projected, label_windows, spat_scale, windows.shape[0], WIN * WIN)
    result = flat_tokens + jnp.dot(mixed, out_weight, precision=highest_precision, preferred_element_type=jnp.float32)
    return from_windows(result.reshape(windows.shape), grid_rows, grid_cols, WIN)
```

```python
import math
import jax, jax.numpy as jnp
from jax import lax
from jax.experimental import pallas as pl
from jax.experimental.pallas import tpu as pltpu

F32, BF16 = jnp.float32, jnp.bfloat16
EPS = 1e-05

def parts(x, n):
    out = []
    for i in range(n):
        p = x.astype(BF16)
        out.append(p)
        if i < n - 1:
            x = x - p.astype(F32)
    return out

def wparts(w, n):
    out = []
    for i in range(n):
        p = lax.reduce_precision(w, 8, 7)
        out.append(p.astype(BF16))
        w = w - p
    return out

def lhs6(x, axis=1):
    a, b, c = parts(x, 3)
    return jnp.concatenate([a, b, c, a, b, a], axis)

def rhs6(w, axis=0):
    a, b, c = wparts(w, 3)
    return jnp.concatenate([a, a, a, b, b, c], axis)

def lhs3(x, axis=1):
    a, b = parts(x, 2)
    return jnp.concatenate([a, b, a], axis)

def rhs3(w, axis=0):
    a, b = wparts(w, 2)
    return jnp.concatenate([a, a, b], axis)

def mm(a, b, ca=1, cb=0):
    return lax.dot_general(a, b, (((ca,), (cb,)), ((), ())), preferred_element_type=F32)

def bd(w):
    z = jnp.zeros_like(w)
    return jnp.concatenate([jnp.concatenate([w, z], 1), jnp.concatenate([z, w], 1)], 0)

def prepare(embed, bpos, qkv, out, sscale, up, down, pool):
    cent = lambda w: w - jnp.mean(w, axis=1, keepdims=True)
    cat = jnp.concatenate
    we = cat([bd(embed), bd(cent(embed))], 1)
    bp = cat([bpos.reshape(56, 128), cent(bpos).reshape(56, 128)], 1)
    qs = jnp.repeat(sscale * (math.log2(math.e) / 4.0), 16)[None, :]
    q, k, v = qkv[:, :64] * qs, qkv[:, 64:128], qkv[:, 128:]
    w1, w2, w3 = wparts(cat([q, k, v, v], 1), 3)
    wq = cat([w1, w1, w2, w2, w1, w3], 0)
    wo = rhs3(cat([bd(out), bd(cent(out))], 1))
    u1, u2 = wparts(up, 2)
    wu = cat([u1, u1, u2, u2], 0)
    d1, d2 = wparts(bd(down), 2)
    wd = cat([cat([d1, d2], 1), cat([d1, jnp.zeros_like(d1)], 1)], 0)
    g = pool.reshape(12, 56, 2).transpose(0, 2, 1)
    e8 = jnp.eye(8, dtype=F32)
    gp = (g[:, :, None, None, :] * e8[None, None, :, :, None]).reshape(192, 448)
    gp = jnp.stack(wparts(gp, 2))
    return (rhs6(we), bp, wq, wo, wu, wd, gp)

def gelu(v):
    return 0.5 * v * (1.0 + jnp.tanh(math.sqrt(2 / math.pi) * (v + 0.044715 * (v * v * v))))

def row_tokens(load, we_ref, bp_ref, wq_ref, wo_ref, wu_ref, wd_ref, gp_ref):
    NP = 8
    cat = jnp.concatenate
    x = cat([load(p) for p in range(NP)], 0)
    bpt = cat([bp_ref[...]] * NP, 0)
    t = mm(lhs6(x), we_ref[...]) + bpt
    tok, tokc = t[:, :128], t[:, 128:]
    r_i = lax.broadcasted_iota(jnp.int32, (128, 128), 0) // 64
    c_i = lax.broadcasted_iota(jnp.int32, (128, 128), 1) // 64
    avg = jnp.where(r_i == c_i, 1.0 / 64, 0.0).astype(BF16)
    avg = cat([avg, avg], 0)
    low = lax.broadcasted_iota(jnp.int32, (448, 128), 1) < 64

    def norm(c):
        var = mm(cat(parts(c * c, 2), 1), avg)
        return c * lax.rsqrt(var + EPS)

    def split_bands(n, k):
        ps = [a.astype(F32) for a in parts(n, k)]
        rs = [pltpu.roll(a, 64, 1) for a in ps]
        pairs = [(0, 1)] + ([(2, 0)] if k == 3 else [])
        b0 = [jnp.where(low, ps[i], rs[j]).astype(BF16) for i, j in pairs]
        b1 = [jnp.where(low, rs[i], ps[j]).astype(BF16) for i, j in pairs]
        return cat([cat([b[0]] + b, 1) for b in (b0, b1)], 0)

    qkv = mm(split_bands(norm(tokc), 3), wq_ref[...])
    lane = lax.broadcasted_iota(jnp.int32, (1, 128), 1)
    lowp = lax.broadcasted_iota(jnp.int32, (112, 128), 1) < 64
    mlow = jnp.where(lane < 64, 1.0, 0.0).astype(BF16)
    mhigh = jnp.where(lane < 64, 0.0, 1.0).astype(BF16)
    hm = [jnp.where((lane // 16) % 4 == h, 1.0, 0.0).astype(BF16) for h in range(4)]
    row128 = lax.broadcasted_iota(jnp.int32, (128, 112), 0)
    mixes = []
    for p in range(NP):
        def both(sl):
            return cat([qkv[56 * p:56 * p + 56, sl], qkv[448 + 56 * p:504 + 56 * p, sl]], 0)
        qk, v = both(slice(0, 128)), both(slice(128, 256))
        kq = pltpu.roll(qk, 64, 1)
        q1, q2, q3 = parts(jnp.where(lowp, qk, kq), 3)
        k1, k2, k3 = parts(jnp.where(lowp, kq, qk), 3)
        kl = k1 * mlow + k2 * mhigh
        lhs = cat([kl, kl, k1 * mlow + k3 * mhigh], 1)
        qc = cat([q1, q2, q3 * mlow + q1 * mhigh], 1)
        pad = jnp.zeros((16, 384), BF16)
        heads = []
        for h in range(4):
            heads += [qc * cat([hm[h]] * 3, 1), pad]
        st = mm(lhs, cat(heads, 0), 1, 1)
        m = jnp.max(st, axis=0, keepdims=True)
        e = jnp.exp2(st - m)
        s = jnp.sum(e, axis=0, keepdims=True)
        e1, e2 = parts(e, 2)
        vt = v.T
        vh = vt.astype(BF16).astype(F32)
        vs = jnp.where(row128 < 64, vh, vt - vh).astype(BF16)
        r = mm(vs, e1)
        r2 = mm(vs[:64], e2)
        inv = 1.0 / s
        ot = []
        for h in range(4):
            sl = slice(128 * h, 128 * h + 128)
            o = r[16 * h:16 * h + 16, sl] + r[64 + 16 * h:80 + 16 * h, sl] + r2[16 * h:16 * h + 16, sl]
            ot.append(o * inv[:, sl])
        mt = cat(ot, 0)
        mt = cat([mt, pltpu.roll(mt, 72, 1)], 0)
        mixes.append(mt.T[:56])
    mix = cat(mixes, 0)
    o = mm(lhs3(mix), wo_ref[...])
    n2 = norm(tokc + o[:, 128:])
    h = gelu(mm(split_bands(n2, 2), wu_ref[...]))
    h1, h2 = parts(h, 2)
    hc = cat([h1[:448], h1[448:], h2[:448], h2[448:]], 1)
    d = mm(hc, wd_ref[...])
    y = tok + o[:, :128] + (d[:, :128] + d[:, 128:])
    y1, y2 = parts(y, 2)
    r = mm(gp_ref[0], cat([y1, y2], 1))
    r = (r[:, :128] + r[:, 128:]) + mm(gp_ref[1], y1)
    lo8 = lax.broadcasted_iota(jnp.int32, (8, 128), 1) < 64
    outs = []
    for j in range(6):
        g = lambda a, b: r[((2 * j + a) * 2 + b) * 8:((2 * j + a) * 2 + b) * 8 + 8]
        outs.append(jnp.where(lo8, g(0, 0) + pltpu.roll(g(0, 1), 64, 1),
                              pltpu.roll(g(1, 0), 64, 1) + g(1, 1)))
    return cat(outs, 1)


def spread_kernel(px, we, bp, wq, wo, wu, wd, gp, out, xbuf, zs, lsem, ssem, rsem, zsem, zrem, fsem, frem):
    nb, nr = lax.axis_size("band"), lax.axis_size("row")
    me, row = lax.axis_index("band"), lax.axis_index("row")
    up = lax.rem(row + nr - 1, nr)
    down = lax.rem(row + 1, nr)
    left = lax.rem(me + nb - 1, nb)
    MESH = pl.DeviceIdType.MESH
    barrier = pltpu.get_barrier_semaphore()
    for k in range(1, nb):
        pl.semaphore_signal(barrier, inc=1, device_id={"band": lax.rem(me + k, nb)}, device_id_type=MESH)
    pl.semaphore_signal(barrier, inc=1, device_id={"row": down}, device_id_type=MESH)

    def own(r):
        return pltpu.make_async_copy(px.at[r, me], xbuf.at[r, pl.ds(me * 56, 56)], lsem.at[r])

    def hop(r, k):
        to = lax.rem(me + k, nb)
        return pltpu.make_async_remote_copy(
            src_ref=px.at[r, to], dst_ref=xbuf.at[r, pl.ds(me * 56, 56)],
            send_sem=ssem.at[r, k], recv_sem=rsem.at[r, k],
            device_id={"band": to}, device_id_type=MESH)

    def rise(r):
        return pltpu.make_async_remote_copy(
            src_ref=zs.at[r], dst_ref=out.at[r + 1, pl.ds(0, 8)],
            send_sem=zsem.at[r], recv_sem=zrem.at[r], device_id={"row": up}, device_id_type=MESH)

    def side(r):
        return pltpu.make_async_remote_copy(
            src_ref=out.at[r, pl.ds(0, 8)], dst_ref=out.at[r, pl.ds(8, 8)],
            send_sem=fsem.at[r], recv_sem=frem.at[r], device_id={"band": left}, device_id_type=MESH)

    def start_own(r, c):
        own(r).start()
        return c
    lax.fori_loop(0, 8, start_own, 0)
    pl.semaphore_wait(barrier, nb)

    def start_row(r, c):
        for k in ORDER:
            hop(r, k).start()
        return c
    lax.fori_loop(0, 8, start_row, 0)

    def one(r, c):
        own(r).wait()
        for k in range(1, nb):
            hop(r, k).wait_recv()
        z = row_tokens(lambda p: xbuf[r, pl.ds(p, 56, stride=8), :], we, bp, wq, wo, wu, wd, gp)

        @pl.when(r < 7)
        def _():
            zs[r] = z
            rise(r).start()

        @pl.when(r == 7)
        def _():
            out[0, 0:8] = z
            side(0).start()

        @pl.when(r > 0)
        def _():
            rise(r - 1).wait_recv()
            side(r).start()
        return c
    lax.fori_loop(0, 8, one, 0)

    def finish(r, c):
        for k in range(1, nb):
            hop(r, k).wait_send()
        side(r).wait()

        @pl.when(r < 7)
        def _():
            rise(r).wait_send()
        return c
    lax.fori_loop(0, 8, finish, 0)


ORDER = (4, 3, 5, 2, 6, 1, 7)


def spread(px, *ws):
    V = pl.BlockSpec(memory_space=pltpu.VMEM)
    D = pltpu.SemaphoreType.DMA
    return pl.pallas_call(
        spread_kernel,
        out_shape=jax.ShapeDtypeStruct((8, 16, 768), F32),
        in_specs=[pl.BlockSpec(memory_space=pl.ANY)] + [V] * 7,
        out_specs=V,
        scratch_shapes=[pltpu.VMEM((8, 448, 128), F32), pltpu.VMEM((8, 8, 768), F32),
                        D((8,)), D((8, 8)), D((8, 8)), D((8,)), D((8,)), D((8,)), D((8,))],
        compiler_params=pltpu.CompilerParams(collective_id=0, has_side_effects=True,
                                             vmem_limit_bytes=40 * 2 ** 20),
        name="spread",
    )(px, *ws)


highest_precision = lax.Precision.HIGHEST


def layer_normalize(values):
    average = jnp.mean(values, axis=-1, keepdims=True)
    centred = values - average
    spread_ = jnp.mean(centred * centred, axis=-1, keepdims=True)
    return centred * lax.rsqrt(spread_ + EPS)


def window_attention(projected, same, spat_scale):
    shaped = projected.reshape(64, 3, 12, 64)
    scores = jnp.einsum("qhd,khd->hqk", shaped[:, 0], shaped[:, 1], precision=highest_precision)
    scores = scores * (spat_scale / math.sqrt(64))[:, None, None]
    scores = jnp.where(same[None], scores, -1e30)
    top = jnp.max(scores, axis=-1, keepdims=True)
    e = jnp.exp(scores - top)
    a = e / jnp.sum(e, axis=-1, keepdims=True)
    return jnp.einsum("hqk,khd->qhd", a, shaped[:, 2], precision=highest_precision).reshape(64, 768)


def on_device(pixels, embed, bpos, qkv, out, sscale, upw, downw, pool, qkv_weight, out_weight, spat_scale, shifts):
    w_qkv = lax.all_gather(qkv_weight, "band", axis=1, tiled=True)
    w_out = lax.all_gather(out_weight, "band", axis=1, tiled=True)
    px = pixels.reshape(8, 8, 8, 7, 128).transpose(0, 1, 3, 2, 4).reshape(8, 8, 56, 128)
    square = spread(px, *prepare(embed, bpos, qkv, out, sscale, upw, downw, pool))
    rolled = lax.dynamic_slice(square, (0, shifts[1], 0), (8, 8, 768))
    row_index = lax.axis_index("row") * 8 + jnp.arange(8, dtype=jnp.int32)
    col_index = lax.axis_index("band") * 8 + jnp.arange(8, dtype=jnp.int32)
    row_region = (row_index >= lax.axis_size("row") * 8 - shifts[0]).astype(jnp.int32)
    col_region = (col_index >= lax.axis_size("band") * 8 - shifts[1]).astype(jnp.int32)
    labels = (2 * row_region[:, None] + col_region[None, :]).reshape(64)
    flat = rolled.reshape(64, 768)
    projected = jnp.dot(layer_normalize(flat), w_qkv, precision=highest_precision)
    mixed = window_attention(projected, labels[:, None] == labels[None, :], spat_scale)
    return (flat + jnp.dot(mixed, w_out, precision=highest_precision)).reshape(8, 8, 768)


def solution(mesh):
    P = jax.sharding.PartitionSpec
    return jax.shard_map(
        on_device,
        mesh=mesh,
        in_specs=(P("row", None, "band"), P(), P(), P(), P(), P(), P(), P(), P(),
                  P(None, "band"), P(None, "band"), P(), P()),
        out_specs=P("row", "band", None),
        check_vma=False,
    )
```

```python
import math
import jax, jax.numpy as jnp
from jax import lax
from jax.experimental import pallas as pl
from jax.experimental.pallas import tpu as pltpu

F32, BF16 = jnp.float32, jnp.bfloat16
EPS = 1e-05

def parts(x, n):
    out = []
    for i in range(n):
        p = x.astype(BF16)
        out.append(p)
        if i < n - 1:
            x = x - p.astype(F32)
    return out

def lhs6(x, axis=1):
    a, b, c = parts(x, 3)
    return jnp.concatenate([a, b, c, a, b, a], axis)

def lhs3(x, axis=1):
    a, b = parts(x, 2)
    return jnp.concatenate([a, b, a], axis)

def mm(a, b, ca=1, cb=0):
    return lax.dot_general(a, b, (((ca,), (cb,)), ((), ())), preferred_element_type=F32)

def bd(w):
    z = jnp.zeros_like(w)
    return jnp.concatenate([jnp.concatenate([w, z], 1), jnp.concatenate([z, w], 1)], 0)

def prepare(embed, bpos_t, qkv, wout, sscale, upw, down_t, pool, bs, we, bp, wq, wo, wu, wd, gp):
    cat = jnp.concatenate
    cent = lambda w: w - jnp.mean(w, axis=1, keepdims=True)

    def put(ref, cols, w, order):
        n = w.shape[0]
        ps = parts(w, max(order) + 1)
        for i, j in enumerate(order):
            ref[n * i:n * i + n, cols] = ps[j]
    e = embed[...]
    put(we, slice(0, 128), bd(e), (0, 0, 0, 1, 1, 2))
    put(we, slice(128, 256), bd(cent(e)), (0, 0, 0, 1, 1, 2))
    b = bpos_t[...].T
    bs[...] = cat([b, cent(b)], 1)
    even, odd = bs[pl.ds(0, 56, stride=2), :], bs[pl.ds(1, 56, stride=2), :]
    bp[...] = cat([even[:, :64], odd[:, :64], even[:, 64:], odd[:, 64:]], 1)
    w = qkv[...]
    lane = lax.broadcasted_iota(jnp.int32, (64, 64), 1) // 16
    qs = jnp.where(lane < 2, jnp.where(lane == 0, sscale[0], sscale[1]), jnp.where(lane == 2, sscale[2], sscale[3]))
    q = w[:, :64] * (qs * (math.log2(math.e) / 4.0))
    put(wq, slice(0, 256), cat([q, w[:, 64:128], w[:, 128:], w[:, 128:]], 1), (0, 0, 1, 1, 0, 2))
    o = wout[...]
    put(wo, slice(0, 128), bd(o), (0, 0, 1))
    put(wo, slice(128, 256), bd(cent(o)), (0, 0, 1))
    put(wu, slice(0, 256), upw[...], (0, 0, 1, 1))
    d = bd(down_t[...].T)
    d1, d2 = parts(d, 2)
    wd[0:512, 0:128] = d1
    wd[512:1024, 0:128] = d1
    wd[0:512, 128:256] = d2
    wd[512:1024, 128:256] = jnp.zeros((512, 128), BF16)
    p1, p2 = parts(pool[...], 2)
    bi = lax.broadcasted_iota(jnp.int32, (112, 448), 0)
    ti = lax.broadcasted_iota(jnp.int32, (112, 448), 1)
    own = lax.broadcasted_iota(jnp.int32, (8, 448), 1) // 56 == lax.broadcasted_iota(jnp.int32, (8, 448), 0)
    for b2 in range(2):
        sel = jnp.where(bi == 2 * (ti % 56) + b2, 1.0, 0.0).astype(BF16)
        for i, p in enumerate((p1, p2)):
            g = mm(p, sel)
            for j in range(0, 12, 2):
                for t in (j, j + 1):
                    rows = jnp.where(own, jnp.broadcast_to(g[t:t + 1], (8, 448)), 0.0)
                    gp[i, pl.ds((t * 2 + b2) * 8, 8), :] = rows.astype(BF16)


def gelu(v):
    return 0.5 * v * (1.0 + jnp.tanh(math.sqrt(2 / math.pi) * (v + 0.044715 * (v * v * v))))

def row_tokens(load, we_ref, bp_ref, wq_ref, wo_ref, wu_ref, wd_ref, gp_ref):
    NP = 8
    cat = jnp.concatenate
    x = cat([load(p) for p in range(NP)], 0)
    bpt = cat([bp_ref[...]] * NP, 0)
    t = mm(lhs6(x), we_ref[...]) + bpt
    tok, tokc = t[:, :128], t[:, 128:]
    r_i = lax.broadcasted_iota(jnp.int32, (128, 128), 0) // 64
    c_i = lax.broadcasted_iota(jnp.int32, (128, 128), 1) // 64
    avg = jnp.where(r_i == c_i, 1.0 / 64, 0.0).astype(BF16)
    avg = cat([avg, avg], 0)
    low = lax.broadcasted_iota(jnp.int32, (448, 128), 1) < 64

    def norm(c):
        var = mm(cat(parts(c * c, 2), 1), avg)
        return c * lax.rsqrt(var + EPS)

    def split_bands(n, k):
        ps = [a.astype(F32) for a in parts(n, k)]
        rs = [pltpu.roll(a, 64, 1) for a in ps]
        pairs = [(0, 1)] + ([(2, 0)] if k == 3 else [])
        b0 = [jnp.where(low, ps[i], rs[j]).astype(BF16) for i, j in pairs]
        b1 = [jnp.where(low, rs[i], ps[j]).astype(BF16) for i, j in pairs]
        return cat([cat([b[0]] + b, 1) for b in (b0, b1)], 0)

    qkv = mm(split_bands(norm(tokc), 3), wq_ref[...])
    lane = lax.broadcasted_iota(jnp.int32, (1, 128), 1)
    lowp = lax.broadcasted_iota(jnp.int32, (112, 128), 1) < 64
    mlow = jnp.where(lane < 64, 1.0, 0.0).astype(BF16)
    mhigh = jnp.where(lane < 64, 0.0, 1.0).astype(BF16)
    hm = [jnp.where((lane // 16) % 4 == h, 1.0, 0.0).astype(BF16) for h in range(4)]
    row128 = lax.broadcasted_iota(jnp.int32, (128, 112), 0)
    mixes = []
    for p in range(NP):
        def both(sl):
            return cat([qkv[56 * p:56 * p + 56, sl], qkv[448 + 56 * p:504 + 56 * p, sl]], 0)
        qk, v = both(slice(0, 128)), both(slice(128, 256))
        kq = pltpu.roll(qk, 64, 1)
        q1, q2, q3 = parts(jnp.where(lowp, qk, kq), 3)
        k1, k2, k3 = parts(jnp.where(lowp, kq, qk), 3)
        kl = k1 * mlow + k2 * mhigh
        lhs = cat([kl, kl, k1 * mlow + k3 * mhigh], 1)
        qc = cat([q1, q2, q3 * mlow + q1 * mhigh], 1)
        pad = jnp.zeros((16, 384), BF16)
        heads = []
        for h in range(4):
            heads += [qc * cat([hm[h]] * 3, 1), pad]
        st = mm(lhs, cat(heads, 0), 1, 1)
        m = jnp.max(st, axis=0, keepdims=True)
        e = jnp.exp2(st - m)
        s = jnp.sum(e, axis=0, keepdims=True)
        e1, e2 = parts(e, 2)
        vt = v.T
        vh = vt.astype(BF16).astype(F32)
        vs = jnp.where(row128 < 64, vh, vt - vh).astype(BF16)
        r = mm(vs, e1)
        r2 = mm(vs[:64], e2)
        inv = 1.0 / s
        ot = []
        for h in range(4):
            sl = slice(128 * h, 128 * h + 128)
            o = r[16 * h:16 * h + 16, sl] + r[64 + 16 * h:80 + 16 * h, sl] + r2[16 * h:16 * h + 16, sl]
            ot.append(o * inv[:, sl])
        mt = cat(ot, 0)
        mt = cat([mt, pltpu.roll(mt, 72, 1)], 0)
        mixes.append(mt.T[:56])
    mix = cat(mixes, 0)
    o = mm(lhs3(mix), wo_ref[...])
    n2 = norm(tokc + o[:, 128:])
    h = gelu(mm(split_bands(n2, 2), wu_ref[...]))
    h1, h2 = parts(h, 2)
    hc = cat([h1[:448], h1[448:], h2[:448], h2[448:]], 1)
    d = mm(hc, wd_ref[...])
    y = tok + o[:, :128] + (d[:, :128] + d[:, 128:])
    y1, y2 = parts(y, 2)
    r = mm(gp_ref[0], cat([y1, y2], 1))
    r = (r[:, :128] + r[:, 128:]) + mm(gp_ref[1], y1)
    lo8 = lax.broadcasted_iota(jnp.int32, (8, 128), 1) < 64
    outs = []
    for j in range(6):
        g = lambda a, b: r[((2 * j + a) * 2 + b) * 8:((2 * j + a) * 2 + b) * 8 + 8]
        outs.append(jnp.where(lo8, g(0, 0) + pltpu.roll(g(0, 1), 64, 1),
                              pltpu.roll(g(1, 0), 64, 1) + g(1, 1)))
    return cat(outs, 1)


def window(square, shifts, scale, wg, out):
    cat = jnp.concatenate
    nb, nr = lax.axis_size("band"), lax.axis_size("row")
    shift = shifts[1]
    zr = square[:, 7:15, :]
    for i in range(1, 7):
        zr = jnp.where(shift == i, square[:, i:i + 8, :], zr)
    zr = zr.reshape(64, 768)
    c = zr - jnp.mean(zr, axis=1, keepdims=True)
    n = c * lax.rsqrt(jnp.mean(c * c, axis=1, keepdims=True) + EPS)
    n1, n2, n3 = parts(n, 3)
    n123, n12 = cat([n1, n2, n3], 0), cat([n1, n2], 0)

    def proj(t, full):
        w = parts(cat([wg[j % 12, j // 12] for j in range(16 * t, 16 * t + 16)], 0), 3 if full else 2)
        if full:
            a, b = mm(n123, w[0], 1, 1), mm(n12, w[1], 1, 1)
            return (a[:64] + (a[64:128] + b[:64])) + (a[128:] + b[64:] + mm(n1, w[2], 1, 1))
        a = mm(n12, w[0], 1, 1)
        return a[:64] + (a[64:] + mm(n1, w[1], 1, 1))

    t_i = lax.broadcasted_iota(jnp.int32, (64, 128), 0)
    q_i = lax.broadcasted_iota(jnp.int32, (64, 128), 1) % 64
    low = lax.broadcasted_iota(jnp.int32, (64, 128), 1) < 64
    row0 = lax.axis_index("row") * 8
    col0 = lax.axis_index("band") * 8

    def region(t):
        r = jnp.where(row0 + t // 8 >= nr * 8 - shifts[0], 2, 0)
        return r + jnp.where(col0 + t % 8 >= nb * 8 - shift, 1, 0)
    same = region(t_i) == region(q_i)
    mixed = []
    for half in range(2):
        q, k, v = proj(half, True), proj(2 + half, True), proj(4 + half, False)
        for i in range(3):
            pair = 3 * half + i
            sl = slice(128 * i, 128 * i + 128)
            qp, kp, vp = q[:, sl], k[:, sl], v[:, sl]
            a1, a2, a3 = parts(cat([jnp.where(low, qp, 0.0), jnp.where(low, 0.0, qp)], 0), 3)
            k1, k2, k3 = parts(kp, 3)
            st = mm(cat([k1, k1, k1, k2, k2, k3], 1), cat([a1, a2, a3, a1, a2, a1], 1), 1, 1)
            f = math.log2(math.e) / 8.0
            st = st * jnp.where(low, scale[2 * pair] * f, scale[2 * pair + 1] * f)
            st = jnp.where(same, st, -1e30)
            e = jnp.exp2(st - jnp.max(st, axis=0, keepdims=True))
            a = e * (1.0 / jnp.sum(e, axis=0, keepdims=True))
            p1, p2 = parts(a.T, 2)
            v1, v2 = parts(vp, 2)
            r = mm(cat([p1, p2], 0), v1)
            r = r[:128] + (r[128:] + mm(p1, v2))
            mixed.append(jnp.where(low, r[:64], r[64:]))
    o1, o2 = parts(cat(mixed, 1), 2)
    o12 = cat([o1, o2], 0)
    for t in range(2):
        w = parts(cat([wg[12 + j % 4, j // 4] for j in range(16 * t, 16 * t + 16)], 0), 2)
        a = mm(o12, w[0], 1, 1)
        res = zr[:, 384 * t:384 * t + 384] + (a[:64] + (a[64:] + mm(o1, w[1], 1, 1)))
        out[:, :, 384 * t:384 * t + 384] = res.reshape(8, 8, 384)


ORDER = (4, 3, 5, 2, 6, 1, 7)
MESH = pl.DeviceIdType.MESH


def block_kernel(px, wcat, embed, bpos_t, qkv, wout, sscale, upw, down_t, pool, scale, shifts, out,
                 bs, we, bp, wq, wo, wu, wd, gp, xbuf, zs, square, wg,
                 lsem, ssem, rsem, zsem, zrem, fsem, frem, osem, ysem, yrem, gsem, grem):
    nb, nr = lax.axis_size("band"), lax.axis_size("row")
    me, row = lax.axis_index("band"), lax.axis_index("row")
    up, down = lax.rem(row + nr - 1, nr), lax.rem(row + 1, nr)
    left = lax.rem(me + nb - 1, nb)
    yl, core = me // 2, lax.rem(me, 2)
    yh, x, zc = lax.rem(row, 2), lax.rem(row // 2, 4), row // 8
    zb = lax.rem(zc, 2)
    y = yh * 4 + yl

    def chip_y(d, c):
        t = lax.rem(y + d + 8, 8)
        return {"band": lax.rem(t, 4) * 2 + c, "row": row - yh + t // 4}

    def chip_x(d):
        return {"band": me, "row": zc * 8 + lax.rem(x + d + 4, 4) * 2 + yh}
    chip_z = {"band": me, "row": row + 8 * (1 - 2 * zb)}
    other = {"band": me + 1 - 2 * core, "row": row}

    def piece(x_, zb_, c_):
        return (lax.rem(x_ + 4, 4) * 2 + zb_) * 2 + c_

    barrier = pltpu.get_barrier_semaphore()

    def greet(to):
        pl.semaphore_signal(barrier, inc=1, device_id=to, device_id_type=MESH)
    for k in range(1, nb):
        greet({"band": lax.rem(me + k, nb), "row": row})
    greet({"band": me, "row": down})
    for c in range(2):
        greet(chip_y(-1, c))
        greet(chip_y(1, c))
    greet(chip_y(-2, 0))
    greet(chip_y(2, 1))
    greet(chip_z)
    greet(chip_x(-1))
    greet(chip_x(1))

    def remote(src, dst, send, recv, to):
        return pltpu.make_async_remote_copy(src_ref=src, dst_ref=dst, send_sem=send, recv_sem=recv,
                                            device_id=to, device_id_type=MESH)

    def own(r):
        return pltpu.make_async_copy(px.at[r, me], xbuf.at[r, pl.ds(me * 56, 56)], lsem.at[r])

    def hop(r, k):
        to = lax.rem(me + k, nb)
        return remote(px.at[r, to], xbuf.at[r, pl.ds(me * 56, 56)], ssem.at[r, k], rsem.at[r, k],
                      {"band": to, "row": row})

    def rise(r):
        return remote(zs.at[r], square.at[r + 1, pl.ds(0, 8)], zsem.at[r], zrem.at[r], {"band": me, "row": up})

    def side(r):
        return remote(square.at[r, pl.ds(0, 8)], square.at[r, pl.ds(8, 8)], fsem.at[r], frem.at[r],
                      {"band": left, "row": row})

    def deal(i, c):
        to = chip_y((1, -1, 2 - 4 * core)[i], c)
        s = piece(x, zb, c)
        return remote(wcat.at[pl.ds(s * 24, 24)], wg.at[s, me], ysem.at[i, c], yrem.at[i, core], to)

    def dealt(i, c):
        b = lax.rem(yl + (3, 1, 2)[i], 4) * 2 + c
        return remote(wcat.at[pl.ds(0, 24)], wg.at[piece(x, zb, core), b], ysem.at[i, c], yrem.at[i, c], other)

    def deal_other(s):
        return remote(wcat.at[pl.ds(s * 24, 24)], wg.at[s, me], ysem.at[3, 0], yrem.at[3, 0], other)
    mine = piece(x, zb, core)
    keep = pltpu.make_async_copy(wcat.at[pl.ds(mine * 24, 24)], wg.at[mine, me], osem)

    def pass_on(s, lo, n, i, to):
        ref = wg.at[s, pl.ds(lo, n)]
        return remote(ref, ref, gsem.at[i], grem.at[i], to)
    zo = 1 - zb
    GOT = {"Z": (0, 0, zo, 0, 8), "M0": (1, -1, zb, 0, 8), "P0": (2, 1, zb, 0, 8), "M1": (3, -1, zo, 0, 8),
           "P1": (4, 1, zo, 0, 8), "RM0": (5, 2, zb, 0, 4), "RP0": (6, 2, zb, 4, 4), "RM1": (7, 2, zo, 0, 4),
           "RP1": (8, 2, zo, 4, 4), "O": (9, 0, zb, 0, 8)}

    def got(name):
        i, dx, z, lo, n = GOT[name]
        return pass_on(piece(x + dx, z, core), lo, n, i, other)

    def to_other(name):
        i, dx, z, lo, n = GOT[name]
        return pass_on(piece(x + dx, z, core), lo, n, 10 + i, other)

    def from_other(name):
        i, dx, z, lo, n = GOT[name]
        return pass_on(piece(x + dx, z, 1 - core), lo, n, 10 + i, other)
    def send(name):
        if name == "Z":
            return pass_on(mine, 0, 8, 0, chip_z)
        if name in ("M0", "M1"):
            return pass_on(piece(x, zb if name == "M0" else zo, core), 0, 8, 1 if name == "M0" else 3, chip_x(1))
        if name in ("P0", "P1"):
            return pass_on(piece(x, zb if name == "P0" else zo, core), 0, 8, 2 if name == "P0" else 4, chip_x(-1))
        z = zb if name[2] == "0" else zo
        if name[1] == "M":
            return pass_on(piece(x - 1, z, core), 0, 4, 5 if name == "RM0" else 7, chip_x(1))
        return pass_on(piece(x + 1, z, core), 4, 4, 6 if name == "RP0" else 8, chip_x(-1))

    def start_own(r, c):
        own(r).start()
        return c
    lax.fori_loop(0, 8, start_own, 0)
    keep.start()
    pl.semaphore_wait(barrier, nb + 9)

    def start_row(r, c):
        for k in ORDER:
            hop(r, k).start()
        return c
    start_row(0, 0)
    for i in range(3):
        for c in range(2):
            deal(i, c).start()
    deal_other(piece(x, zb, 1 - core)).start()
    lax.fori_loop(1, 8, start_row, 0)
    prepare(embed, bpos_t, qkv, wout, sscale, upw, down_t, pool, bs, we, bp, wq, wo, wu, wd, gp)

    def weights(step):
        if step == 0:
            keep.wait()
            for i in range(3):
                for c in range(2):
                    dealt(i, c).wait_recv()
            remote(wcat.at[pl.ds(0, 24)], wg.at[mine, me + 1 - 2 * core], ysem.at[3, 0], yrem.at[3, 0], other).wait_recv()
            for name in ("Z", "M0", "P0"):
                send(name).start()
            to_other("O").start()
        if step == 2:
            got("Z").wait_recv()
            send("M1").start()
            send("P1").start()
            to_other("Z").start()
        if step == 3:
            for name, relay in (("M0", "RM0"), ("P0", "RP0")):
                got(name).wait_recv()
                send(relay).start()
                to_other(name).start()
        if step == 5:
            for name, relay in (("M1", "RM1"), ("P1", "RP1")):
                got(name).wait_recv()
                send(relay).start()
                to_other(name).start()
        if step == 6:
            for name in ("RM0", "RP0"):
                got(name).wait_recv()
                to_other(name).start()
        if step == 8:
            for name in ("RM1", "RP1"):
                got(name).wait_recv()
                to_other(name).start()

    def one(r, c):
        own(r).wait()
        for k in range(1, nb):
            hop(r, k).wait_recv()
        z = row_tokens(lambda p: xbuf[r, pl.ds(p, 56, stride=8), :], we, bp, wq, wo, wu, wd, gp)

        @pl.when(r < 7)
        def _():
            zs[r] = z
            rise(r).start()

        @pl.when(r == 7)
        def _():
            square[0, 0:8] = z
            side(0).start()

        @pl.when(r > 0)
        def _():
            rise(r - 1).wait_recv()
            side(r).start()
        for step in (0, 2, 3, 5, 6):
            @pl.when(r == step)
            def _():
                weights(step)
        return c
    lax.fori_loop(0, 8, one, 0)
    weights(8)

    def arrived(r, c):
        side(r).wait_recv()
        return c
    lax.fori_loop(0, 8, arrived, 0)
    for name in GOT:
        from_other(name).wait_recv()
    window(square, shifts, scale, wg, out)

    def finish(r, c):
        for k in range(1, nb):
            hop(r, k).wait_send()
        side(r).wait_send()

        @pl.when(r < 7)
        def _():
            rise(r).wait_send()
        return c
    lax.fori_loop(0, 8, finish, 0)
    for i in range(3):
        for c in range(2):
            deal(i, c).wait_send()
    deal_other(piece(x, zb, 1 - core)).wait_send()
    for name in GOT:
        to_other(name).wait_send()
        if name != "O":
            send(name).wait_send()


def block(*args):
    V, S, A = (pl.BlockSpec(memory_space=m) for m in (pltpu.VMEM, pltpu.SMEM, pl.ANY))
    D = pltpu.SemaphoreType.DMA
    B = lambda *s: pltpu.VMEM(s, BF16)
    M = lambda *s: pltpu.VMEM(s, F32)
    return pl.pallas_call(
        block_kernel,
        out_shape=jax.ShapeDtypeStruct((8, 8, 768), F32),
        in_specs=[A, A, V, V, V, V, S, V, V, V, S, S],
        out_specs=V,
        scratch_shapes=[M(112, 128), B(768, 256), M(56, 256), B(384, 256), B(384, 256), B(256, 256),
                        B(1024, 256), B(2, 192, 448),
                        M(8, 448, 128), M(8, 8, 768), M(8, 16, 768), M(16, 8, 24, 768),
                        D((8,)), D((8, 8)), D((8, 8)), D((8,)), D((8,)), D((8,)), D((8,)), D,
                        D((4, 2)), D((4, 2)), D((20,)), D((20,))],
        compiler_params=pltpu.CompilerParams(collective_id=0, has_side_effects=True,
                                             vmem_limit_bytes=56 * 2 ** 20),
        name="block",
    )(*args)


def on_device(pixels, embed, bpos, qkv, wout, sscale, upw, down, pool, qkv_weight, out_weight, spat_scale, shifts):
    px = pixels.reshape(8, 8, 8, 7, 128).transpose(0, 1, 3, 2, 4).reshape(8, 8, 56, 128)
    wcat = jnp.concatenate([qkv_weight.T, out_weight.T], 0)
    return block(px, wcat, embed, bpos.T, qkv, wout, sscale, upw, down.T, pool, spat_scale, shifts)


def solution(mesh):
    P = jax.sharding.PartitionSpec
    return jax.shard_map(
        on_device,
        mesh=mesh,
        in_specs=(P("row", None, "band"), P(), P(), P(), P(), P(), P(), P(), P(),
                  P(None, "band"), P(None, "band"), P(), P()),
        out_specs=P("row", "band", None),
        check_vma=False,
    )
```
